1024 devices in a mesh: sub: 64 (over y, z), crs: 16 (over x, core).
Axes of the slice: x: 8, y: 8, z: 8, core: 2. Of those that a mesh axis runs over, the one named last changes fastest.
Arguments:
- jump_data: float32 [64, 16, 6, 384], P('sub', 'crs'), may hold values from -6 to 6
- lumped_scale: float32 [64, 16, 384], P('sub', 'crs'), may hold values from 0.3 to 3
- schur_inverse: float32 [64, 16, 768, 768], P('sub', 'crs'), as said below
- coarse_coupling: float32 [64, 16, 24, 768], P('sub', 'crs'), may hold values from -0.4375 to 0.4375
- corner_inverse: float32 [4096, 4096], P(None, 'crs'), as said below
- own_dof: int32 [64, 16, 384], P('sub', 'crs'), may hold values from 0 to 767, as said below
- nbr_dof: int32 [64, 16, 384], P('sub', 'crs'), may hold values from 0 to 767, as said below
- live_count: int32 [64, 16], P('sub', 'crs'), may hold values from 1 to 384, as said below
- corner_index: int32 [64, 16, 24], P('sub', 'crs'), may hold values from 0 to 4095
Outputs:
- multipliers: float32 [64, 16, 6, 384], P('sub', 'crs')
- residual: float32 [64, 16, 6, 384], P('sub', 'crs')
The draws below stay inside these ranges and needn't reach their ends.
Inputs may be any that keep to these rules, and one draw needn't show every extreme that they name: `own_dof`: the 384 entries of one subdomain are distinct. `nbr_dof`: the 384 entries of one subdomain are distinct. `live_count`: some subdomain has all 384 slots live. `schur_inverse`: symmetric positive definite. `corner_inverse`: symmetric positive definite.
All inputs are finite; a program needn't handle non-finite values.
Results may differ from the reference program's by a relative error of at most 0.00021.
Values sent between devices are 32-bit elements; how exact they have to be, the bound alone decides.
A program may use at most 32 MiB of HBM per device.

```python
import math
import jax
import jax.numpy as jnp
from jax import lax

IFACE = 768
LAM = 384
NCS = 24
CASES = 6
ITERS = 2
CHAIN = 64
SLABS = 16
NCORNER = 4096


def draw_schur_inverse(key, part):
    first, second = jax.random.split(jax.random.fold_in(key, 11))
    raw = jax.random.normal(first, (CHAIN, SLABS, IFACE, IFACE), jnp.float32)
    sym = (raw + jnp.swapaxes(raw, -1, -2)) * (0.25 / IFACE ** 0.5)
    diag = jax.random.uniform(second, (CHAIN, SLABS, IFACE), jnp.float32, 1.0, 2.0)
    return sym + diag[..., :, None] * jnp.eye(IFACE, dtype=jnp.float32)


def draw_corner_inverse(key, part):
    first, second = jax.random.split(jax.random.fold_in(key, 23))
    raw = jax.random.normal(first, (NCORNER, NCORNER), jnp.float32)
    sym = (raw + raw.T) * (0.25 / NCORNER ** 0.5)
    diag = jax.random.uniform(second, (NCORNER,), jnp.float32, 1.0, 2.0)
    return sym + jnp.diag(diag)


def draw_slots(key, salt):
    keys = jax.random.split(jax.random.fold_in(key, salt), CHAIN * SLABS)
    picks = jax.vmap(lambda k: jax.random.permutation(k, IFACE)[:LAM])(keys)
    return picks.reshape(CHAIN, SLABS, LAM).astype(jnp.int32)


def draw_own_dof(key, part):
    return draw_slots(key, 31)


def draw_nbr_dof(key, part):
    return draw_slots(key, 37)


def draw_live_count(key, part):
    first, second, third = jax.random.split(jax.random.fold_in(key, 41), 3)
    left = jax.random.randint(first, (CHAIN, SLABS), 0, LAM)
    right = jax.random.randint(second, (CHAIN, SLABS), 0, LAM)
    counts = 1 + left * right // LAM
    where_full = jax.random.randint(third, (), 0, CHAIN * SLABS)
    places = jnp.arange(CHAIN * SLABS, dtype=jnp.int32).reshape(CHAIN, SLABS)
    return jnp.where(places == where_full, LAM, counts).astype(jnp.int32)


def plant(array, rng, low, largest):
    place = [jax.random.randint(jax.random.fold_in(rng, axis), (), 0, length) for axis, length in enumerate(array.shape)]
    longest = array.shape.index(max(array.shape))
    beside = place[:longest] + [(place[longest] + 1) % array.shape[longest]] + place[longest + 1:]
    return array.at[tuple(place)].set(low).at[tuple(beside)].set(largest)


def block_scale(key, extent, cuts, smallest, top_value):
    gain = 1.0
    for dim, blocks in cuts:
        steps = jax.random.uniform(jax.random.fold_in(jax.random.fold_in(key, 6), dim), (blocks,), jnp.float32, smallest / len(cuts), top_value / len(cuts))
        gain = gain * jnp.repeat(jnp.exp(steps), extent[dim] // blocks).reshape((-1,) + (1,) * (len(extent) - 1 - dim))
    return gain


def normal_values(key, extent, scale, reach, cuts=(), kind=jnp.bfloat16):
    entries = jax.random.normal(key, extent, jnp.float32) * scale
    if len(cuts) > 0:
        entries = block_scale(key, extent, cuts, -0.22, 0.18) * entries
    return jnp.clip(entries, min=-reach, max=reach).astype(kind)


def setup_inputs(seed: int = 0) -> dict:
    key_of = jax.random.split(jax.random.key(seed), 10)
    return {
        "jump_data": normal_values(key_of[0], (CHAIN, SLABS, CASES, LAM), 1.0, 6.0, ((0, 64), (1, 16)), jnp.float32),
        "lumped_scale": jnp.clip(jnp.exp(math.log(3.0) - 2.3025851 * jax.random.uniform(key_of[1], (CHAIN, SLABS, LAM), jnp.float32) ** block_scale(key_of[1], (CHAIN, SLABS, LAM), ((0, 64), (1, 16)), -0.2, 0.2)), 0.3, 3.0),
        "schur_inverse": draw_schur_inverse(jax.random.fold_in(key_of[9], 71), 0),
        "coarse_coupling": normal_values(key_of[3], (CHAIN, SLABS, NCS, IFACE), (IFACE // 4) ** -0.5, 0.4375, ((0, 64), (1, 16)), jnp.float32),
        "corner_inverse": draw_corner_inverse(jax.random.fold_in(key_of[9], 71), 0),
        "own_dof": draw_own_dof(jax.random.fold_in(key_of[9], 71), 0),
        "nbr_dof": draw_nbr_dof(jax.random.fold_in(key_of[9], 71), 0),
        "live_count": draw_live_count(jax.random.fold_in(key_of[9], 71), 0),
        "corner_index": plant(jax.random.randint(key_of[8], (CHAIN, SLABS, NCS), 0, NCORNER), jax.random.fold_in(key_of[8], 1), 0, NCORNER - 1).astype(jnp.int32),
    }


def spread_rows(values, index):
    return jax.vmap(lambda v, i: jnp.zeros((CASES, IFACE), jnp.float32).at[:, i].add(v))(values, index)


def pick_rows(values, index):
    return jax.vmap(lambda v, i: v[:, i])(values, index)


def reference(jump_data, lumped_scale, schur_inverse, coarse_coupling, corner_inverse, own_dof, nbr_dof, live_count, corner_index):
    highest = lax.Precision.HIGHEST
    count = CHAIN * SLABS
    live = (jnp.arange(LAM, dtype=jnp.int32)[None, None, :] < live_count[:, :, None]).astype(jnp.float32)
    live_flat = live.reshape(count, LAM)
    own_flat = own_dof.reshape(count, LAM)
    nbr_flat = nbr_dof.reshape(count, LAM)
    flat_corner = corner_index.reshape(count * NCS)

    def operate(field):
        masked = field.reshape(count, CASES, LAM) * live_flat[:, None, :]
        own_load = spread_rows(masked, own_flat).reshape(CHAIN, SLABS, CASES, IFACE)
        next_load = spread_rows(masked, nbr_flat).reshape(CHAIN, SLABS, CASES, IFACE)
        load = own_load - jnp.roll(next_load, 1, axis=0)
        local_part = jnp.einsum("csij,csjk->csik", load, schur_inverse, precision=highest)
        corner_force = jnp.einsum("csij,csnj->csin", load, coarse_coupling, precision=highest)
        moved = jnp.transpose(corner_force, (2, 0, 1, 3)).reshape(CASES, count * NCS)
        corner_total = jnp.zeros((CASES, NCORNER), jnp.float32).at[:, flat_corner].add(moved)
        corner_solution = jnp.dot(corner_total, corner_inverse, precision=highest)
        picked = jnp.transpose(corner_solution[:, corner_index], (1, 2, 0, 3))
        displacement = local_part + jnp.einsum("csin,csnj->csij", picked, coarse_coupling, precision=highest)
        here = displacement.reshape(count, CASES, IFACE)
        beyond = jnp.roll(displacement, -1, axis=0).reshape(count, CASES, IFACE)
        image = (pick_rows(here, own_flat) - pick_rows(beyond, nbr_flat)) * live_flat[:, None, :]
        return image.reshape(CHAIN, SLABS, CASES, LAM)

    def inner(left, right):
        return jnp.sum(left * right, axis=(0, 1, 3))

    scale = lumped_scale[:, :, None, :]
    residual = jump_data * live[:, :, None, :]
    multipliers = jnp.zeros_like(residual)
    precon = scale * residual
    direction = precon
    norm_now = inner(residual, precon)
    for step in range(ITERS):
        image = operate(direction)
        alpha = (norm_now / inner(direction, image))[None, None, :, None]
        multipliers = multipliers + alpha * direction
        residual = residual - alpha * image
        if step + 1 < ITERS:
            precon = scale * residual
            norm_next = inner(residual, precon)
            direction = precon + (norm_next / norm_now)[None, None, :, None] * direction
            norm_now = norm_next
    return multipliers, residual
```

```python
import functools

import jax
import jax.numpy as jnp
from jax import lax
from jax.experimental import pallas as pl
from jax.experimental.pallas import tpu as pltpu
from jax.sharding import Mesh
from jax.sharding import PartitionSpec as P

MESH = pl.DeviceIdType.MESH
LANES = 128
ROWS = 8
F32 = jnp.float32
BF16 = jnp.bfloat16
CONTRACT_LAST = (((1,), (1,)), ((), ()))
CONTRACT = (((1,), (0,)), ((), ()))


def parts(value):
    high = value.astype(BF16).astype(F32)
    rest = value - high
    middle = rest.astype(BF16).astype(F32)
    low = rest - middle
    return jnp.concatenate([high, middle, low], axis=0).astype(BF16)


def times(value, matrices, dims):
    rows = value.shape[0]
    stacked = parts(value)
    total = None
    for matrix in matrices:
        found = lax.dot_general(stacked, matrix, dims, preferred_element_type=F32)
        total = found if total is None else total + found
    return total[:rows] + total[rows : 2 * rows] + total[2 * rows :]


def store_split(value, high_ref, low_ref):
    high = value.astype(BF16)
    high_ref[...] = high
    low_ref[...] = (value - high.astype(F32)).astype(BF16)


def kernel(
    ny,
    nz,
    nx,
    nk,
    given_ref,
    scale_ref,
    coupling_ref,
    own_ref,
    nbr_ref,
    index_ref,
    live_ref,
    schur_hbm,
    inverse_hbm,
    mult_ref,
    res_ref,
    schur,
    inverse,
    schur_high,
    schur_low,
    own_map,
    next_map,
    corner_map,
    rows_of,
    rows_high,
    rows_low,
    own_wide,
    pair_wide,
    pair_high,
    pair_low,
    index_pad,
    index_right,
    index_mine,
    index_line,
    index_rows,
    index_smem,
    coupling_right,
    load_send,
    load_recv,
    disp_send,
    disp_recv,
    force_send,
    force_recv,
    pick_send,
    pick_recv,
    sum_y0,
    sum_z0,
    sum_y1,
    sum_z1,
    local_sem,
    near_send,
    near_recv,
    index_send_sem,
    index_recv_sem,
    force_send_sem,
    force_recv_sem,
    pick_send_sem,
    pick_recv_sem,
    y_send_sem,
    y_recv_sem,
    z_send_sem,
    z_recv_sem,
):
    y, z, x, k = (lax.axis_index(a) for a in ("y", "z", "x", "k"))
    slab = x * nk + k
    slabs = nx * nk
    iface = coupling_ref.shape[1]
    corners = coupling_ref.shape[0]
    records = given_ref.shape[1]
    block = inverse.shape[1]
    half = LANES // nk

    def plus(value, step, count):
        return lax.rem(value + step + count, count)

    right_z = plus(z, 1, nz)
    right_y = plus(y, jnp.where(z == nz - 1, 1, 0), ny)
    left_z = plus(z, -1, nz)
    left_y = plus(y, jnp.where(z == 0, -1, 0), ny)
    right = {"y": right_y, "z": right_z}
    left = {"y": left_y, "z": left_z}

    def by_distance(count):
        return sorted(range(1, count), key=lambda d: -min(d, count - d))

    line = []
    for dx in sorted(range(nx), key=lambda d: -min(d, nx - d)):
        for dk in range(nk):
            if dx or dk:
                line.append((plus(x, dx, nx), plus(k, dk, nk)))
    ys = [plus(y, d, ny) for d in by_distance(ny)]
    zs = [plus(z, d, nz) for d in by_distance(nz)]

    barrier = pltpu.get_barrier_semaphore()
    everyone = [{"x": px, "k": pk} for px, pk in line]
    everyone += [{"y": py} for py in ys] + [{"z": pz} for pz in zs] + [left, right]
    for peer in everyone:
        pl.semaphore_signal(barrier, inc=1, device_id=peer, device_id_type=MESH)

    get_schur = pltpu.make_async_copy(schur_hbm, schur, local_sem.at[0])
    get_inverse = pltpu.make_async_copy(inverse_hbm, inverse, local_sem.at[1])
    get_schur.start()
    get_inverse.start()

    started = []

    def send(source, target, send_sem, recv_sem, device):
        copy = pltpu.make_async_remote_copy(
            src_ref=source,
            dst_ref=target,
            send_sem=send_sem,
            recv_sem=recv_sem,
            device_id=device,
            device_id_type=MESH,
        )
        copy.start()
        started.append(copy)

    def arrive(target, send_sem, recv_sem, device):
        pltpu.make_async_remote_copy(
            src_ref=target,
            dst_ref=target,
            send_sem=send_sem,
            recv_sem=recv_sem,
            device_id=device,
            device_id_type=MESH,
        ).wait_recv()

    def spread_line(sources, target, send_sem, recv_sem):
        for slot, (px, pk) in enumerate(line):
            send(sources(px), target.at[slab], send_sem.at[slot], recv_sem.at[slab], {"x": px, "k": pk})

    def await_line(target, send_sem, recv_sem):
        for px, pk in line:
            peer = px * nk + pk
            arrive(target.at[peer], send_sem.at[0], recv_sem.at[peer], {"x": px, "k": pk})

    def spread_axis(buffer, axis, me, peers, send_sem, recv_sem):
        for slot, peer in enumerate(peers):
            send(buffer.at[me], buffer.at[me], send_sem.at[slot], recv_sem.at[me], {axis: peer})

    def await_axis(buffer, axis, peers, send_sem, recv_sem):
        for peer in peers:
            arrive(buffer.at[peer], send_sem.at[0], recv_sem.at[peer], {axis: peer})

    def added(buffer, count):
        total = buffer[0]
        for slot in range(1, count):
            total = total + buffer[slot]
        return total

    def padded(value):
        return jnp.concatenate([value, jnp.zeros((ROWS - value.shape[0], value.shape[1]), F32)], axis=0)

    live_row = lax.broadcasted_iota(jnp.int32, (1, records), 1) < live_ref[0, 0]
    residual0 = padded(given_ref[...]) * live_row.astype(F32)
    scale = scale_ref[...]
    direction0 = residual0 * scale
    rows_iface = lax.broadcasted_iota(jnp.int32, (iface, records), 0)
    own_map[...] = jnp.where((rows_iface == own_ref[...]) & live_row, 1.0, 0.0).astype(BF16)
    next_map[...] = jnp.where((rows_iface == nbr_ref[...]) & live_row, 1.0, 0.0).astype(BF16)
    load_send[0] = times(direction0, (next_map[...],), CONTRACT_LAST)
    index_pad[...] = jnp.full((ROWS, LANES), -1, jnp.int32)
    index_pad[0:1, 0:corners] = index_ref[...]

    pl.semaphore_wait(barrier, len(everyone))

    send(load_send.at[0], load_recv.at[0], near_send.at[0], near_recv.at[0], right)
    send(index_pad, index_right, near_send.at[1], near_recv.at[1], left)
    send(coupling_ref, coupling_right, near_send.at[2], near_recv.at[2], left)

    own_load0 = times(direction0, (own_map[...],), CONTRACT_LAST)
    own_wide[...] = jnp.zeros_like(own_wide)
    pair_wide[...] = jnp.zeros_like(pair_wide)
    rows_of[...] = jnp.zeros_like(rows_of)
    first = pl.multiple_of(k * half, 8)
    second = pl.multiple_of(k * half + corners, 8)
    coupling = coupling_ref[...]
    own_wide[pl.ds(first, corners), :] = coupling
    wide_high = own_wide[...].astype(BF16)
    wide_low = (own_wide[...] - wide_high.astype(F32)).astype(BF16)
    pair_wide[pl.ds(first, corners), :] = times(coupling, (own_map[...],), CONTRACT)

    arrive(index_right, near_send.at[1], near_recv.at[1], right)
    lane = lax.broadcasted_iota(jnp.int32, (ROWS, LANES), 1)
    both = jnp.where(lane < corners, index_pad[...], pltpu.roll(index_right[...], corners, 1))
    both = jnp.where(lane < 2 * corners, both, -1)
    for other in range(1, nk):
        both = jnp.where(k == other, pltpu.roll(both, other * half, 1), both)
    index_mine[...] = both
    spread_line(lambda px: index_mine, index_line, index_send_sem, index_recv_sem)

    arrive(load_recv.at[0], near_send.at[0], near_recv.at[0], left)
    load0 = own_load0 - load_recv[0]
    force = times(load0, (wide_high, wide_low), CONTRACT_LAST)
    force_send[0] = force
    spread_line(lambda px: force_send.at[0], force_recv.at[0], force_send_sem.at[0], force_recv_sem.at[0])

    get_schur.wait()
    store_split(schur[...], schur_high, schur_low)
    disp0 = times(load0, (schur_high[...], schur_low[...]), CONTRACT)
    disp_send[0] = disp0
    send(disp_send.at[0], disp_recv.at[0], near_send.at[3], near_recv.at[3], left)
    arrive(coupling_right, near_send.at[2], near_recv.at[2], right)
    pair_wide[pl.ds(second, corners), :] = -times(coupling_right[...], (next_map[...],), CONTRACT)
    store_split(pair_wide[...], pair_high, pair_low)

    await_line(index_line, index_send_sem, index_recv_sem)
    index_line[slab] = index_mine[...]
    block_rows = lax.broadcasted_iota(jnp.int32, (block, LANES), 0) + slab * block
    for px in range(nx):
        row = index_line[px * nk]
        for pk in range(1, nk):
            row = jnp.maximum(row, index_line[px * nk + pk])
        row = row[0:1]
        index_rows[px : px + 1, :] = row
        corner_map[:, px * LANES : (px + 1) * LANES] = jnp.where(block_rows == row, 1.0, 0.0).astype(BF16)
    to_smem = pltpu.make_async_copy(index_rows, index_smem, local_sem.at[2])
    to_smem.start()

    def line_force(step):
        force_recv[step, slab] = force_send[step]
        tiles = []
        for px in range(nx):
            tile = force_recv[step, px * nk]
            for pk in range(1, nk):
                tile = tile + force_recv[step, px * nk + pk]
            tiles.append(tile)
        return jnp.concatenate(tiles, axis=1)

    def send_picks(step, picks):
        for px in range(nx):
            pick_send[step, px] = picks[:, px * LANES : (px + 1) * LANES]
        pick_recv[step, slab] = pick_send[step, x]
        spread_line(
            lambda px: pick_send.at[step, px], pick_recv.at[step], pick_send_sem.at[step], pick_recv_sem.at[step]
        )

    def get_picks(step):
        await_line(pick_recv.at[step], pick_send_sem.at[step], pick_recv_sem.at[step])
        return added(pick_recv.at[step], slabs)

    await_line(force_recv.at[0], force_send_sem.at[0], force_recv_sem.at[0])
    sum_y0[y] = times(line_force(0), (corner_map[...],), CONTRACT_LAST)
    spread_axis(sum_y0, "y", y, ys, y_send_sem.at[0], y_recv_sem.at[0])

    get_inverse.wait()
    to_smem.wait()

    def take(j, carry):
        for px in range(nx):
            for pk in range(nk):
                at = index_smem[px, pk * half + j]
                rows_of[pl.ds(px * LANES + pk * half + j, 1), :] = inverse[pl.ds(at, 1), :]
        return carry

    lax.fori_loop(0, 2 * corners, take, 0)
    store_split(rows_of[...], rows_high, rows_low)

    await_axis(sum_y0, "y", ys, y_send_sem.at[0], y_recv_sem.at[0])
    sum_z0[z] = added(sum_y0, ny)
    spread_axis(sum_z0, "z", z, zs, z_send_sem.at[0], z_recv_sem.at[0])
    arrive(disp_recv.at[0], near_send.at[3], near_recv.at[3], right)
    local0 = times(disp0, (own_map[...],), CONTRACT) - times(disp_recv[0], (next_map[...],), CONTRACT)
    await_axis(sum_z0, "z", zs, z_send_sem.at[0], z_recv_sem.at[0])
    total0 = added(sum_z0, nz)
    send_picks(0, times(total0, (rows_high[...], rows_low[...]), CONTRACT_LAST))
    solved0 = get_picks(0)
    image0 = local0 + times(solved0, (pair_high[...], pair_low[...]), CONTRACT)

    scaled = image0 * scale
    load_send[1] = times(scaled, (next_map[...],), CONTRACT_LAST)
    send(load_send.at[1], load_recv.at[1], near_send.at[4], near_recv.at[4], right)
    force_send[1] = times(scaled, (pair_high[...], pair_low[...]), CONTRACT_LAST)
    spread_line(lambda px: force_send.at[1], force_recv.at[1], force_send_sem.at[1], force_recv_sem.at[1])
    own_load1 = times(scaled, (own_map[...],), CONTRACT_LAST)

    def inner(first_value, second_value):
        return jnp.sum(first_value * second_value, axis=1, keepdims=True)

    start_norm = inner(residual0, direction0)
    curvature = inner(direction0, image0)
    scaled_norm = inner(image0, scaled)
    arrive(load_recv.at[1], near_send.at[4], near_recv.at[4], left)
    load1 = own_load1 - load_recv[1]
    disp1 = times(load1, (schur_high[...], schur_low[...]), CONTRACT)
    disp_send[1] = disp1
    send(disp_send.at[1], disp_recv.at[1], near_send.at[5], near_recv.at[5], left)
    energy = inner(load1, disp1)
    sums = jnp.where(
        lane == 0,
        start_norm,
        jnp.where(lane == 1, curvature, jnp.where(lane == 2, scaled_norm, jnp.where(lane == 3, energy, 0.0))),
    )
    await_line(force_recv.at[1], force_send_sem.at[1], force_recv_sem.at[1])
    forces = line_force(1)
    sum_y1[y, :, 0:block] = times(forces, (corner_map[...],), CONTRACT_LAST)
    sum_y1[y, :, block : 2 * block] = times(forces, (rows_high[...], rows_low[...]), CONTRACT)
    sum_y1[y, :, 2 * block :] = sums
    spread_axis(sum_y1, "y", y, ys, y_send_sem.at[1], y_recv_sem.at[1])
    await_axis(sum_y1, "y", ys, y_send_sem.at[1], y_recv_sem.at[1])
    sum_z1[z] = added(sum_y1, ny)
    spread_axis(sum_z1, "z", z, zs, z_send_sem.at[1], z_recv_sem.at[1])
    arrive(disp_recv.at[1], near_send.at[5], near_recv.at[5], right)
    local1 = times(disp1, (own_map[...],), CONTRACT) - times(disp_recv[1], (next_map[...],), CONTRACT)
    await_axis(sum_z1, "z", zs, z_send_sem.at[1], z_recv_sem.at[1])
    total1 = added(sum_z1, nz)
    solved_block = total1[:, block : 2 * block]
    sums = total1[:, 2 * block :]
    sums = sums + jnp.where(lane == 3, inner(total1[:, 0:block], solved_block), 0.0)
    picks = times(solved_block, (corner_map[...],), CONTRACT)
    sums = pltpu.roll(sums, LANES - half // 4, 1)
    send_picks(1, picks + jnp.concatenate([sums] * nx, axis=1))
    solved1 = get_picks(1)
    image1 = local1 + times(solved1, (pair_high[...], pair_low[...]), CONTRACT)

    at = LANES - half // 4
    norm0 = solved1[:, at : at + 1]
    alpha0 = norm0 / solved1[:, at + 1 : at + 2]
    norm1 = alpha0 * alpha0 * solved1[:, at + 2 : at + 3] - norm0
    ratio = norm1 / norm0
    bent = alpha0 * alpha0 * solved1[:, at + 3 : at + 4] - (norm0 + norm1) * (1.0 + ratio) / alpha0
    alpha1 = norm1 / bent
    residual1 = residual0 - alpha0 * image0
    direction1 = residual1 * scale + ratio * direction0
    along1 = image0 - alpha0 * image1 + ratio * image0
    cases = mult_ref.shape[0]
    mult_ref[...] = (alpha0 * direction0 + alpha1 * direction1)[0:cases]
    res_ref[...] = (residual1 - alpha1 * along1)[0:cases]

    for copy in started:
        copy.wait_send()


def per_device(ny, nz, nx, nk, jump_data, lumped_scale, schur_inverse, coarse_coupling, corner_inverse, own_dof, nbr_dof, live_count, corner_index):
    cases, records = jump_data.shape[2:]
    corners, iface = coarse_coupling.shape[2:]
    total, block = corner_inverse.shape
    slabs = nx * nk
    wide = nx * LANES
    vmem = lambda *shape: pltpu.VMEM(shape, F32)
    half = lambda *shape: pltpu.VMEM(shape, BF16)
    whole = lambda *shape: pltpu.VMEM(shape, jnp.int32)
    sem = lambda *shape: pltpu.SemaphoreType.DMA(shape)
    in_vmem = pl.BlockSpec(memory_space=pltpu.VMEM)
    scratch = [
        vmem(iface, iface),
        vmem(total, block),
        half(iface, iface),
        half(iface, iface),
        half(iface, records),
        half(iface, records),
        half(block, wide),
        vmem(wide, block),
        half(wide, block),
        half(wide, block),
        vmem(LANES, iface),
        vmem(LANES, records),
        half(LANES, records),
        half(LANES, records),
        whole(ROWS, LANES),
        whole(ROWS, LANES),
        whole(ROWS, LANES),
        whole(slabs, ROWS, LANES),
        whole(nx, LANES),
        pltpu.SMEM((nx, LANES), jnp.int32),
        vmem(corners, iface),
        vmem(2, ROWS, iface),
        vmem(2, ROWS, iface),
        vmem(2, ROWS, iface),
        vmem(2, ROWS, iface),
        vmem(2, ROWS, LANES),
        vmem(2, slabs, ROWS, LANES),
        vmem(2, nx, ROWS, LANES),
        vmem(2, slabs, ROWS, LANES),
        vmem(ny, ROWS, block),
        vmem(nz, ROWS, block),
        vmem(ny, ROWS, 2 * block + LANES),
        vmem(nz, ROWS, 2 * block + LANES),
        sem(3),
        sem(6),
        sem(6),
        sem(slabs),
        sem(slabs),
        sem(2, slabs),
        sem(2, slabs),
        sem(2, slabs),
        sem(2, slabs),
        sem(2, ny),
        sem(2, ny),
        sem(2, nz),
        sem(2, nz),
    ]
    outs = pl.pallas_call(
        functools.partial(kernel, ny, nz, nx, nk),
        out_shape=(jax.ShapeDtypeStruct((cases, records), F32),) * 2,
        in_specs=[in_vmem] * 6
        + [pl.BlockSpec(memory_space=pltpu.SMEM), pl.BlockSpec(memory_space=pl.ANY), pl.BlockSpec(memory_space=pl.ANY)],
        out_specs=(in_vmem, in_vmem),
        scratch_shapes=scratch,
        compiler_params=pltpu.CompilerParams(collective_id=0, has_side_effects=True, vmem_limit_bytes=40 * 1024 * 1024),
        name="solve",
    )(
        jump_data[0, 0],
        lumped_scale[0],
        coarse_coupling[0, 0],
        own_dof[0],
        nbr_dof[0],
        corner_index[0],
        live_count,
        schur_inverse[0, 0],
        corner_inverse,
    )
    return outs[0][None, None], outs[1][None, None]


def solution(mesh):
    devices = mesh.devices
    sub, crs = devices.shape
    side = 8 if sub == 64 else 2
    ny, nz, nx, nk = side, sub // side, crs // 2, 2
    finer = Mesh(devices.reshape(ny, nz, nx, nk), ("y", "z", "x", "k"))
    SUB, CRS = ("y", "z"), ("x", "k")
    placed = (
        P(SUB, CRS, None, None),
        P(SUB, CRS, None),
        P(SUB, CRS, None, None),
        P(SUB, CRS, None, None),
        P(None, CRS),
        P(SUB, CRS, None),
        P(SUB, CRS, None),
        P(SUB, CRS),
        P(SUB, CRS, None),
    )
    return jax.shard_map(
        functools.partial(per_device, ny, nz, nx, nk),
        mesh=finer,
        in_specs=placed,
        out_specs=(P(SUB, CRS, None, None), P(SUB, CRS, None, None)),
        check_vma=False,
    )
```

```python
import functools

import jax
import jax.numpy as jnp
from jax import lax
from jax.experimental import pallas as pl
from jax.experimental.pallas import tpu as pltpu
from jax.sharding import Mesh
from jax.sharding import PartitionSpec as P

MESH = pl.DeviceIdType.MESH
LANES = 128
ROWS = 8
F32 = jnp.float32
BF16 = jnp.bfloat16
CONTRACT_LAST = (((1,), (1,)), ((), ()))
CONTRACT = (((1,), (0,)), ((), ()))


def parts(value):
    high = value.astype(BF16).astype(F32)
    rest = value - high
    middle = rest.astype(BF16).astype(F32)
    low = rest - middle
    return jnp.concatenate([high, middle, low], axis=0).astype(BF16)


def times(value, matrices, dims):
    rows = value.shape[0]
    stacked = parts(value)
    total = None
    for matrix in matrices:
        found = lax.dot_general(stacked, matrix, dims, preferred_element_type=F32)
        total = found if total is None else total + found
    return total[:rows] + total[rows : 2 * rows] + total[2 * rows :]


def store_split(value, high_ref, low_ref):
    high = value.astype(BF16)
    high_ref[...] = high
    low_ref[...] = (value - high.astype(F32)).astype(BF16)


def kernel(
    ny,
    nz,
    nx,
    nk,
    given_hbm,
    scale_hbm,
    coupling_hbm,
    own_hbm,
    nbr_hbm,
    index_hbm,
    live_ref,
    schur_hbm,
    inverse_hbm,
    mult_hbm,
    res_hbm,
    given_ref,
    scale_ref,
    coupling_ref,
    own_ref,
    nbr_ref,
    index_ref,
    mult_ref,
    res_ref,
    schur,
    inverse,
    schur_high,
    schur_low,
    own_map,
    next_map,
    corner_map,
    rows_of,
    rows_high,
    rows_low,
    own_wide,
    pair_wide,
    pair_high,
    pair_low,
    index_pad,
    index_right,
    index_mine,
    index_line,
    index_rows,
    index_smem,
    coupling_right,
    load_send,
    load_recv,
    disp_send,
    disp_recv,
    force_send,
    force_recv,
    pick_send,
    pick_recv,
    sum_y0,
    sum_z0,
    first_y,
    first_z,
    second_z,
    second_y,
    local_sem,
    near_send,
    near_recv,
    line_send,
    line_recv,
    axis_send,
    axis_recv,
    relay_sem,
):
    y, z, x, k = (lax.axis_index(a) for a in ("y", "z", "x", "k"))
    slab = x * nk + k
    slabs = nx * nk
    iface = coupling_ref.shape[1]
    corners = coupling_ref.shape[0]
    cases, _, records = given_ref.shape
    block = inverse.shape[1]
    half = LANES // nk

    def plus(value, step, count):
        return lax.rem(value + step + count, count)

    right_z = plus(z, 1, nz)
    right_y = plus(y, jnp.where(z == nz - 1, 1, 0), ny)
    left_z = plus(z, -1, nz)
    left_y = plus(y, jnp.where(z == 0, -1, 0), ny)
    right = {"y": right_y, "z": right_z}
    left = {"y": left_y, "z": left_z}

    def by_distance(count):
        return sorted(range(1, count), key=lambda d: -min(d, count - d))

    line = []
    for dx in sorted(range(nx), key=lambda d: -min(d, nx - d)):
        for dk in range(nk):
            if dx or dk:
                line.append((plus(x, dx, nx), plus(k, dk, nk)))
    ys = [plus(y, d, ny) for d in by_distance(ny)]
    zs = [plus(z, d, nz) for d in by_distance(nz)]

    aside = {
        "x": [{"x": plus(x, d, nx), "k": pk} for d in (-1, 1) for pk in range(nk)],
        "y": [{"y": plus(y, d, ny)} for d in (-1, 1)],
        "z": [{"z": plus(z, d, nz)} for d in (-1, 1)],
    }
    partners = [{"k": plus(k, d, nk)} for d in range(1, nk)]
    barrier = pltpu.get_barrier_semaphore()
    greeted = [left, right] + aside["x"] + aside["y"] + aside["z"] + partners
    for peer in greeted:
        pl.semaphore_signal(barrier, inc=1, device_id=peer, device_id_type=MESH)

    def relay_signal(axis, step):
        for peer in aside[axis]:
            pl.semaphore_signal(relay_sem.at["xyz".index(axis), step], inc=1, device_id=peer, device_id_type=MESH)

    def relay_wait(axis, step):
        pl.semaphore_wait(relay_sem.at["xyz".index(axis), step], len(aside[axis]))

    def relay(axis, count, first_step, last_step):
        for step in range(first_step, last_step):
            if step < count // 2 - 1:
                relay_wait(axis, step)
                if step + 1 < count // 2 - 1:
                    relay_signal(axis, step + 1)

    def fetch(source, target, slot):
        copy = pltpu.make_async_copy(source, target, local_sem.at[slot])
        copy.start()
        return copy

    get_nbr = fetch(nbr_hbm, nbr_ref, 3)
    get_given = fetch(given_hbm, given_ref, 4)
    get_scale = fetch(scale_hbm, scale_ref, 5)
    get_index = fetch(index_hbm, index_ref, 6)
    get_own = fetch(own_hbm, own_ref, 7)
    get_coupling = fetch(coupling_hbm, coupling_ref, 8)
    get_schur = fetch(schur_hbm, schur, 0)
    get_inverse = fetch(inverse_hbm, inverse, 1)

    unsent = []

    def send(source, target, send_sem, recv_sem, device):
        pltpu.make_async_remote_copy(
            src_ref=source,
            dst_ref=target,
            send_sem=send_sem,
            recv_sem=recv_sem,
            device_id=device,
            device_id_type=MESH,
        ).start()

    def bytes_of(view, send_sem, recv_sem):
        return pltpu.make_async_remote_copy(
            src_ref=view,
            dst_ref=view,
            send_sem=send_sem,
            recv_sem=recv_sem,
            device_id=right,
            device_id_type=MESH,
        )

    def send_near(source, target, slot, device):
        send(source, target, near_send.at[slot], near_recv.at[slot], device)
        unsent.append(bytes_of(source, near_send.at[slot], near_recv.at[slot]))

    def await_near(target, slot):
        bytes_of(target, near_send.at[slot], near_recv.at[slot]).wait_recv()

    def spread_line(source_of, target, rows, slot):
        for px, pk in line:
            send(
                source_of(px, pk),
                target.at[slab, 0:rows],
                line_send.at[slot],
                line_recv.at[slot],
                {"x": px, "k": pk},
            )
        unsent.append(bytes_of(target.at[0 : slabs - 1, 0:rows], line_send.at[slot], line_recv.at[slot]))

    def await_line(target, rows, slot):
        bytes_of(target.at[0 : slabs - 1, 0:rows], line_send.at[slot], line_recv.at[slot]).wait_recv()

    def spread_axis(buffer, axis, slot):
        me, peers = (y, ys) if axis == "y" else (z, zs)
        for peer in peers:
            send(buffer.at[me], buffer.at[me], axis_send.at[slot], axis_recv.at[slot], {axis: peer})
        unsent.append(bytes_of(buffer.at[0 : len(peers)], axis_send.at[slot], axis_recv.at[slot]))

    def await_axis(buffer, axis, slot):
        peers = ys if axis == "y" else zs
        bytes_of(buffer.at[0 : len(peers)], axis_send.at[slot], axis_recv.at[slot]).wait_recv()

    def added(buffer, count):
        total = buffer[0]
        for slot in range(1, count):
            total = total + buffer[slot]
        return total

    def padded(value):
        return jnp.concatenate([value, jnp.zeros((ROWS - value.shape[0], value.shape[1]), F32)], axis=0)

    live_row = lax.broadcasted_iota(jnp.int32, (1, records), 1) < live_ref[0, 0]
    rows_iface = lax.broadcasted_iota(jnp.int32, (iface, records), 0)
    get_nbr.wait()
    get_given.wait()
    get_scale.wait()
    given = jnp.concatenate([given_ref[i] for i in range(cases)], axis=0)
    residual0 = padded(given) * live_row.astype(F32)
    scale = scale_ref[...]
    direction0 = residual0 * scale
    next_map[...] = jnp.where((rows_iface == nbr_ref[...]) & live_row, 1.0, 0.0).astype(BF16)
    load_send[0] = times(direction0, (next_map[...],), CONTRACT_LAST)
    get_index.wait()
    index_pad[...] = jnp.full((ROWS, LANES), -1, jnp.int32)
    index_pad[0:1, 0:corners] = index_ref[...]

    get_own.wait()
    get_coupling.wait()
    pl.semaphore_wait(barrier, len(greeted))
    for axis, count in (("x", nx), ("y", ny), ("z", nz)):
        if count // 2 > 1:
            relay_signal(axis, 0)

    send_near(load_send.at[0], load_recv.at[0], 0, right)
    send_near(index_pad, index_right, 1, left)
    send_near(coupling_ref, coupling_right, 2, left)
    relay("x", nx, 0, 1)

    own_map[...] = jnp.where((rows_iface == own_ref[...]) & live_row, 1.0, 0.0).astype(BF16)
    own_load0 = times(direction0, (own_map[...],), CONTRACT_LAST)
    own_wide[...] = jnp.zeros_like(own_wide)
    pair_wide[...] = jnp.zeros_like(pair_wide)
    rows_of[...] = jnp.zeros_like(rows_of)
    coupling = coupling_ref[...]
    own_pair = times(coupling, (own_map[...],), CONTRACT)
    for at in range(0, LANES, half):
        own_wide[at : at + corners, :] = coupling
        pair_wide[at : at + corners, :] = own_pair
    wide_high = own_wide[...].astype(BF16)
    wide_low = (own_wide[...] - wide_high.astype(F32)).astype(BF16)
    relay("x", nx, 1, nx)

    await_near(index_right, 1)
    lane = lax.broadcasted_iota(jnp.int32, (ROWS, LANES), 1)
    row = lax.broadcasted_iota(jnp.int32, (ROWS, LANES), 0)
    low = lane < half
    both = jnp.where(lane < corners, index_pad[...], pltpu.roll(index_right[...], corners, 1))
    both = jnp.where(lane < 2 * corners, both, -1)
    index_mine[...] = jnp.where(low, both, pltpu.roll(both, half, 1))
    spread_line(lambda px, pk: index_mine.at[0:1], index_line, 1, 0)

    packed = cases // 2

    def up(tile):
        return pltpu.roll(tile, ROWS - packed, 0)

    def unpacked(tile):
        below = jnp.where((row < packed) & low, tile, 0.0)
        return jnp.where((row >= packed) & (row < cases) & ~low, pltpu.roll(tile, packed, 0), below)

    def send_force(step, force):
        force_send[step] = jnp.where(low, force, up(force))
        spread_line(lambda px, pk: force_send.at[step, 0:packed], force_recv.at[step], packed, 1 + 2 * step)

    await_near(load_recv.at[0], 0)
    load0 = own_load0 - load_recv[0]
    force = times(load0, (wide_high, wide_low), CONTRACT_LAST)
    send_force(0, force)
    relay("y", ny, 0, 1)
    relay("z", nz, 0, 1)

    get_schur.wait()
    store_split(schur[...], schur_high, schur_low)
    disp0 = times(load0, (schur_high[...], schur_low[...]), CONTRACT)
    disp_send[0] = disp0
    send_near(disp_send.at[0], disp_recv.at[0], 3, left)
    relay("y", ny, 1, ny)
    relay("z", nz, 1, 2)
    await_near(coupling_right, 2)
    next_pair = -times(coupling_right[...], (next_map[...],), CONTRACT)
    for at in range(corners, LANES, half):
        pair_wide[at : at + corners, :] = next_pair
    store_split(pair_wide[...], pair_high, pair_low)

    await_line(index_line, 1, 0)
    index_line[slab] = index_mine[...]
    block_rows = lax.broadcasted_iota(jnp.int32, (block, LANES), 0) + slab * block
    for px in range(nx):
        found = jnp.where(low, index_line[px * nk], index_line[px * nk + 1])[0:1]
        index_rows[px : px + 1, :] = found
        corner_map[:, px * LANES : (px + 1) * LANES] = jnp.where(block_rows == found, 1.0, 0.0).astype(BF16)
    to_smem = pltpu.make_async_copy(index_rows, index_smem, local_sem.at[2])
    to_smem.start()

    def line_force(step):
        await_line(force_recv.at[step], packed, 1 + 2 * step)
        force_recv[step, slab] = force_send[step]
        tiles = []
        for px in range(nx):
            even, odd = force_recv[step, px * nk], force_recv[step, px * nk + 1]
            upper = jnp.where(low, even, pltpu.roll(odd, half, 1))
            lower = pltpu.roll(jnp.where(low, pltpu.roll(even, half, 1), odd), packed, 0)
            tiles.append(jnp.where(row < packed, upper, jnp.where(row < cases, lower, 0.0)))
        return jnp.concatenate(tiles, axis=1)

    def send_picks(step, picks):
        for px in range(nx):
            tile = picks[:, px * LANES : (px + 1) * LANES]
            above = up(tile)
            pick_send[step, px, 0] = jnp.where(low, tile, pltpu.roll(above, half, 1))
            pick_send[step, px, 1] = jnp.where(low, pltpu.roll(tile, half, 1), above)
        spread_line(lambda px, pk: pick_send.at[step, px, pk, 0:packed], pick_recv.at[step], packed, 2 + 2 * step)
        pick_recv[step, slab] = pick_send[step, x, k]

    def get_picks(step):
        await_line(pick_recv.at[step], packed, 2 + 2 * step)
        return unpacked(added(pick_recv.at[step], slabs))

    sum_y0[y] = times(line_force(0), (corner_map[...],), CONTRACT_LAST)
    spread_axis(sum_y0, "y", 0)

    get_inverse.wait()
    to_smem.wait()

    def take(j, carry):
        for px in range(nx):
            for pk in range(nk):
                at = index_smem[px, pk * half + j]
                rows_of[pl.ds(px * LANES + pk * half + j, 1), :] = inverse[pl.ds(at, 1), :]
        return carry

    lax.fori_loop(0, 2 * corners, take, 0)
    store_split(rows_of[...], rows_high, rows_low)

    relay("z", nz, 2, nz)
    await_axis(sum_y0, "y", 0)
    sum_z0[z] = added(sum_y0, ny)
    spread_axis(sum_z0, "z", 1)
    await_near(disp_recv.at[0], 3)
    local0 = times(disp0, (own_map[...],), CONTRACT) - times(disp_recv[0], (next_map[...],), CONTRACT)
    await_axis(sum_z0, "z", 1)
    total0 = added(sum_z0, nz)
    send_picks(0, times(total0, (rows_high[...], rows_low[...]), CONTRACT_LAST))
    solved0 = get_picks(0)
    image0 = local0 + times(solved0, (pair_high[...], pair_low[...]), CONTRACT)

    scaled = image0 * scale
    load_send[1] = times(scaled, (next_map[...],), CONTRACT_LAST)
    send_near(load_send.at[1], load_recv.at[1], 4, right)
    send_force(1, times(scaled, (pair_high[...], pair_low[...]), CONTRACT_LAST))
    own_load1 = times(scaled, (own_map[...],), CONTRACT_LAST)

    def inner(first_value, second_value):
        return jnp.sum(first_value * second_value, axis=1, keepdims=True)

    start_norm = inner(residual0, direction0)
    curvature = inner(direction0, image0)
    scaled_norm = inner(image0, scaled)
    await_near(load_recv.at[1], 4)
    load1 = own_load1 - load_recv[1]
    disp1 = times(load1, (schur_high[...], schur_low[...]), CONTRACT)
    disp_send[1] = disp1
    send_near(disp_send.at[1], disp_recv.at[1], 5, left)
    energy = inner(load1, disp1)
    sums = jnp.where(
        lane == 0,
        start_norm,
        jnp.where(lane == 1, curvature, jnp.where(lane == 2, scaled_norm, jnp.where(lane == 3, energy, 0.0))),
    )
    forces = line_force(1)
    first_y[y, :, 0:block] = times(forces, (corner_map[...],), CONTRACT_LAST)
    first_y[y, :, block:] = sums
    spread_axis(first_y, "y", 2)
    first_z[z] = times(forces, (rows_high[...], rows_low[...]), CONTRACT)
    spread_axis(first_z, "z", 3)
    await_near(disp_recv.at[1], 5)
    local1 = times(disp1, (own_map[...],), CONTRACT) - times(disp_recv[1], (next_map[...],), CONTRACT)
    await_axis(first_y, "y", 2)
    second_z[z] = added(first_y, ny)
    spread_axis(second_z, "z", 4)
    await_axis(first_z, "z", 3)
    second_y[y] = added(first_z, nz)
    spread_axis(second_y, "y", 5)
    await_axis(second_y, "y", 5)
    solved_block = added(second_y, ny)
    picks = times(solved_block, (corner_map[...],), CONTRACT)
    await_axis(second_z, "z", 4)
    total1 = added(second_z, nz)
    sums = total1[:, block:]
    sums = sums + jnp.where(lane == 3, inner(total1[:, 0:block], solved_block), 0.0)
    spare = half - 16
    sums = pltpu.roll(sums, spare, 1) + pltpu.roll(sums, half + spare, 1)
    send_picks(1, picks + jnp.concatenate([sums] * nx, axis=1))
    solved1 = get_picks(1)
    image1 = local1 + times(solved1, (pair_high[...], pair_low[...]), CONTRACT)

    sums = solved1 + pltpu.roll(solved1, half, 1)
    norm0, curvature, scaled_norm, energy = (sums[:, spare + i : spare + i + 1] for i in range(4))
    alpha0 = norm0 / curvature
    norm1 = alpha0 * alpha0 * scaled_norm - norm0
    ratio = norm1 / norm0
    bent = alpha0 * alpha0 * energy - (norm0 + norm1) * (1.0 + ratio) / alpha0
    alpha1 = norm1 / bent
    residual1 = residual0 - alpha0 * image0
    direction1 = residual1 * scale + ratio * direction0
    along1 = image0 - alpha0 * image1 + ratio * image0
    mult = alpha0 * direction0 + alpha1 * direction1
    res = residual1 - alpha1 * along1
    for i in range(cases):
        mult_ref[i] = mult[i : i + 1]
        res_ref[i] = res[i : i + 1]
    puts = [fetch(mult_ref, mult_hbm, 9), fetch(res_ref, res_hbm, 10)]
    for put in puts:
        put.wait()

    for copy in unsent:
        copy.wait_send()


def per_device(ny, nz, nx, nk, jump_data, lumped_scale, schur_inverse, coarse_coupling, corner_inverse, own_dof, nbr_dof, live_count, corner_index):
    cases, records = jump_data.shape[2:]
    corners, iface = coarse_coupling.shape[2:]
    total, block = corner_inverse.shape
    slabs = nx * nk
    wide = nx * LANES
    vmem = lambda *shape: pltpu.VMEM(shape, F32)
    half = lambda *shape: pltpu.VMEM(shape, BF16)
    whole = lambda *shape: pltpu.VMEM(shape, jnp.int32)
    sem = lambda *shape: pltpu.SemaphoreType.DMA(shape)
    in_hbm = pl.BlockSpec(memory_space=pltpu.HBM)
    scratch = [
        vmem(cases, 1, records),
        vmem(1, records),
        vmem(corners, iface),
        whole(1, records),
        whole(1, records),
        whole(1, corners),
        vmem(cases, 1, records),
        vmem(cases, 1, records),
        vmem(iface, iface),
        vmem(total, block),
        half(iface, iface),
        half(iface, iface),
        half(iface, records),
        half(iface, records),
        half(block, wide),
        vmem(wide, block),
        half(wide, block),
        half(wide, block),
        vmem(LANES, iface),
        vmem(LANES, records),
        half(LANES, records),
        half(LANES, records),
        whole(ROWS, LANES),
        whole(ROWS, LANES),
        whole(ROWS, LANES),
        whole(slabs, ROWS, LANES),
        whole(nx, LANES),
        pltpu.SMEM((nx, LANES), jnp.int32),
        vmem(corners, iface),
        vmem(2, ROWS, iface),
        vmem(2, ROWS, iface),
        vmem(2, ROWS, iface),
        vmem(2, ROWS, iface),
        vmem(2, ROWS, LANES),
        vmem(2, slabs, ROWS, LANES),
        vmem(2, nx, nk, ROWS, LANES),
        vmem(2, slabs, ROWS, LANES),
        vmem(ny, ROWS, block),
        vmem(nz, ROWS, block),
        vmem(ny, ROWS, block + LANES),
        vmem(nz, ROWS, block),
        vmem(nz, ROWS, block + LANES),
        vmem(ny, ROWS, block),
        sem(11),
        sem(6),
        sem(6),
        sem(5),
        sem(5),
        sem(6),
        sem(6),
        pltpu.SemaphoreType.REGULAR((3, 4)),
    ]
    outs = pl.pallas_call(
        functools.partial(kernel, ny, nz, nx, nk),
        out_shape=(jax.ShapeDtypeStruct((cases, 1, records), F32),) * 2,
        in_specs=[in_hbm] * 6 + [pl.BlockSpec(memory_space=pltpu.SMEM)] + [in_hbm] * 2,
        out_specs=(in_hbm, in_hbm),
        scratch_shapes=scratch,
        compiler_params=pltpu.CompilerParams(collective_id=0, has_side_effects=True, vmem_limit_bytes=67043328),
        name="solve",
    )(
        jnp.transpose(jump_data[0], (1, 0, 2)),
        lumped_scale[0],
        coarse_coupling[0, 0],
        own_dof[0],
        nbr_dof[0],
        corner_index[0],
        live_count,
        schur_inverse[0, 0],
        corner_inverse,
    )
    return tuple(jnp.transpose(out, (1, 0, 2))[None] for out in outs)


def solution(mesh):
    devices = mesh.devices
    sub, crs = devices.shape
    side = 8 if sub == 64 else 2
    ny, nz, nx, nk = side, sub // side, crs // 2, 2
    finer = Mesh(devices.reshape(ny, nz, nx, nk), ("y", "z", "x", "k"))
    SUB, CRS = ("y", "z"), ("x", "k")
    placed = (
        P(SUB, CRS, None, None),
        P(SUB, CRS, None),
        P(SUB, CRS, None, None),
        P(SUB, CRS, None, None),
        P(None, CRS),
        P(SUB, CRS, None),
        P(SUB, CRS, None),
        P(SUB, CRS),
        P(SUB, CRS, None),
    )
    return jax.shard_map(
        functools.partial(per_device, ny, nz, nx, nk),
        mesh=finer,
        in_specs=placed,
        out_specs=(P(SUB, CRS, None, None), P(SUB, CRS, None, None)),
        check_vma=False,
    )
```

```python
import functools

import jax
import jax.numpy as jnp
from jax import lax
from jax.experimental import pallas as pl
from jax.experimental.pallas import tpu as pltpu
from jax.sharding import Mesh
from jax.sharding import PartitionSpec as P

MESH = pl.DeviceIdType.MESH
LANES = 128
ROWS = 8
F32 = jnp.float32
BF16 = jnp.bfloat16
CONTRACT_LAST = (((1,), (1,)), ((), ()))
CONTRACT = (((1,), (0,)), ((), ()))


def parts(value):
    high = value.astype(BF16).astype(F32)
    rest = value - high
    middle = rest.astype(BF16).astype(F32)
    low = rest - middle
    return jnp.concatenate([high, middle, low], axis=0).astype(BF16)


def times(value, matrices, dims):
    rows = value.shape[0]
    stacked = parts(value)
    total = None
    for matrix in matrices:
        found = lax.dot_general(stacked, matrix, dims, preferred_element_type=F32)
        total = found if total is None else total + found
    return total[:rows] + total[rows : 2 * rows] + total[2 * rows :]


def store_split(value, high_ref, low_ref):
    high = value.astype(BF16)
    high_ref[...] = high
    low_ref[...] = (value - high.astype(F32)).astype(BF16)


def kernel(
    ny,
    nz,
    nx,
    nk,
    given_hbm,
    scale_hbm,
    coupling_hbm,
    own_hbm,
    nbr_hbm,
    index_hbm,
    live_ref,
    schur_hbm,
    inverse_hbm,
    out_hbm,
    given_ref,
    scale_ref,
    coupling_ref,
    own_ref,
    nbr_ref,
    index_ref,
    out_ref,
    schur,
    inverse,
    schur_high,
    schur_low,
    own_map,
    next_map,
    corner_map,
    rows_of,
    rows_high,
    rows_low,
    own_wide,
    pair_wide,
    pair_high,
    pair_low,
    index_pad,
    index_right,
    index_mine,
    index_line,
    index_rows,
    index_smem,
    coupling_right,
    load_send,
    load_recv,
    disp_send,
    disp_recv,
    force_send,
    force_recv,
    pick_send,
    pick_recv,
    sum_y0,
    sum_z0,
    first_y,
    first_z,
    second_z,
    second_y,
    local_sem,
    near_send,
    near_recv,
    line_send,
    line_recv,
    axis_send,
    axis_recv,
    relay_sem,
):
    y, z, x, k = (lax.axis_index(a) for a in ("y", "z", "x", "k"))
    slab = x * nk + k
    slabs = nx * nk
    iface = coupling_ref.shape[1]
    corners = coupling_ref.shape[0]
    cases, _, records = given_ref.shape
    block = inverse.shape[1]
    half = LANES // nk

    def plus(value, step, count):
        return lax.rem(value + step + count, count)

    right_z = plus(z, 1, nz)
    right_y = plus(y, jnp.where(z == nz - 1, 1, 0), ny)
    left_z = plus(z, -1, nz)
    left_y = plus(y, jnp.where(z == 0, -1, 0), ny)
    right = {"y": right_y, "z": right_z}
    left = {"y": left_y, "z": left_z}

    def by_distance(count):
        return sorted(range(1, count), key=lambda d: -min(d, count - d))

    line = []
    for dx in sorted(range(nx), key=lambda d: -min(d, nx - d)):
        for dk in range(nk):
            if dx or dk:
                line.append((plus(x, dx, nx), plus(k, dk, nk)))
    ys = [plus(y, d, ny) for d in by_distance(ny)]
    zs = [plus(z, d, nz) for d in by_distance(nz)]

    aside = {
        "x": [{"x": plus(x, d, nx), "k": pk} for d in (-1, 1) for pk in range(nk)],
        "y": [{"y": plus(y, d, ny)} for d in (-1, 1)],
        "z": [{"z": plus(z, d, nz)} for d in (-1, 1)],
    }
    partners = [{"k": plus(k, d, nk)} for d in range(1, nk)]
    barrier = pltpu.get_barrier_semaphore()
    greeted = [left, right] + aside["x"] + aside["y"] + aside["z"] + partners
    for peer in greeted:
        pl.semaphore_signal(barrier, inc=1, device_id=peer, device_id_type=MESH)

    def relay_signal(axis, step):
        for peer in aside[axis]:
            pl.semaphore_signal(relay_sem.at["xyz".index(axis), step], inc=1, device_id=peer, device_id_type=MESH)

    def relay_wait(axis, step):
        pl.semaphore_wait(relay_sem.at["xyz".index(axis), step], len(aside[axis]))

    def relay(axis, count, first_step, last_step):
        for step in range(first_step, last_step):
            if step < count // 2 - 1:
                relay_wait(axis, step)
                if step + 1 < count // 2 - 1:
                    relay_signal(axis, step + 1)

    def fetch(source, target, slot):
        copy = pltpu.make_async_copy(source, target, local_sem.at[slot])
        copy.start()
        return copy

    get_nbr = fetch(nbr_hbm, nbr_ref, 3)
    get_given = fetch(given_hbm, given_ref, 4)
    get_scale = fetch(scale_hbm, scale_ref, 5)
    get_index = fetch(index_hbm, index_ref, 6)
    get_own = fetch(own_hbm, own_ref, 7)
    get_coupling = fetch(coupling_hbm, coupling_ref, 8)
    get_schur = fetch(schur_hbm, schur, 0)
    get_inverse = fetch(inverse_hbm, inverse, 1)

    unsent = []

    def send(source, target, send_sem, recv_sem, device):
        pltpu.make_async_remote_copy(
            src_ref=source,
            dst_ref=target,
            send_sem=send_sem,
            recv_sem=recv_sem,
            device_id=device,
            device_id_type=MESH,
        ).start()

    def bytes_of(view, send_sem, recv_sem):
        return pltpu.make_async_remote_copy(
            src_ref=view,
            dst_ref=view,
            send_sem=send_sem,
            recv_sem=recv_sem,
            device_id=right,
            device_id_type=MESH,
        )

    def send_near(source, target, slot, device):
        send(source, target, near_send.at[slot], near_recv.at[slot], device)
        unsent.append(bytes_of(source, near_send.at[slot], near_recv.at[slot]))

    def await_near(target, slot):
        bytes_of(target, near_send.at[slot], near_recv.at[slot]).wait_recv()

    def spread_line(source_of, target, rows, slot):
        for px, pk in line:
            send(
                source_of(px, pk),
                target.at[slab, 0:rows],
                line_send.at[slot],
                line_recv.at[slot],
                {"x": px, "k": pk},
            )
        unsent.append(bytes_of(target.at[0 : slabs - 1, 0:rows], line_send.at[slot], line_recv.at[slot]))

    def await_line(target, rows, slot):
        bytes_of(target.at[0 : slabs - 1, 0:rows], line_send.at[slot], line_recv.at[slot]).wait_recv()

    def spread_axis(buffer, axis, slot):
        me, peers = (y, ys) if axis == "y" else (z, zs)
        for peer in peers:
            send(buffer.at[me, 0:cases], buffer.at[me, 0:cases], axis_send.at[slot], axis_recv.at[slot], {axis: peer})
        unsent.append(bytes_of(buffer.at[0 : len(peers), 0:cases], axis_send.at[slot], axis_recv.at[slot]))

    def await_axis(buffer, axis, slot):
        peers = ys if axis == "y" else zs
        bytes_of(buffer.at[0 : len(peers), 0:cases], axis_send.at[slot], axis_recv.at[slot]).wait_recv()

    def added(buffer, count):
        total = buffer[0]
        for slot in range(1, count):
            total = total + buffer[slot]
        return total

    def padded(value):
        return jnp.concatenate([value, jnp.zeros((ROWS - value.shape[0], value.shape[1]), F32)], axis=0)

    rows_iface = lax.broadcasted_iota(jnp.int32, (iface, records), 0)
    live_row = lax.broadcasted_iota(jnp.int32, (1, records), 1) < live_ref[0, 0]
    get_nbr.wait()
    get_given.wait()
    get_scale.wait()
    given = jnp.concatenate([given_ref[i] for i in range(cases)], axis=0)
    residual0 = padded(given) * live_row.astype(F32)
    scale = scale_ref[...]
    direction0 = residual0 * scale
    next_map[...] = jnp.where((rows_iface == nbr_ref[...]) & live_row, 1.0, 0.0).astype(BF16)
    load_send[0] = times(direction0, (next_map[...],), CONTRACT_LAST)
    get_index.wait()
    index_pad[...] = jnp.full((ROWS, LANES), -1, jnp.int32)
    index_pad[0:1, 0:corners] = index_ref[...]

    get_own.wait()
    get_coupling.wait()
    pl.semaphore_wait(barrier, len(greeted))
    for axis, count in (("x", nx), ("y", ny), ("z", nz)):
        if count // 2 > 1:
            relay_signal(axis, 0)

    send_near(load_send.at[0, 0:cases], load_recv.at[0, 0:cases], 0, right)
    send_near(index_pad.at[0:1], index_right.at[0:1], 1, left)
    send_near(coupling_ref, coupling_right, 2, left)
    relay("x", nx, 0, 1)

    own_map[...] = jnp.where((rows_iface == own_ref[...]) & live_row, 1.0, 0.0).astype(BF16)
    own_load0 = times(direction0, (own_map[...],), CONTRACT_LAST)
    own_wide[...] = jnp.zeros_like(own_wide)
    pair_wide[...] = jnp.zeros_like(pair_wide)
    rows_of[...] = jnp.zeros_like(rows_of)
    coupling = coupling_ref[...]
    own_pair = times(coupling, (own_map[...],), CONTRACT)
    for at in range(0, LANES, half):
        own_wide[at : at + corners, :] = coupling
        pair_wide[at : at + corners, :] = own_pair
    wide_high = own_wide[...].astype(BF16)
    wide_low = (own_wide[...] - wide_high.astype(F32)).astype(BF16)
    relay("x", nx, 1, nx)

    await_near(index_right.at[0:1], 1)
    lane = lax.broadcasted_iota(jnp.int32, (ROWS, LANES), 1)
    row = lax.broadcasted_iota(jnp.int32, (ROWS, LANES), 0)
    low = lane < half
    both = jnp.where(lane < corners, index_pad[...], pltpu.roll(index_right[...], corners, 1))
    both = jnp.where(lane < 2 * corners, both, -1)
    index_mine[...] = jnp.where(low, both, pltpu.roll(both, half, 1))
    spread_line(lambda px, pk: index_mine.at[0:1], index_line, 1, 0)

    packed = cases // 2

    def up(tile):
        return pltpu.roll(tile, ROWS - packed, 0)

    def unpacked(tile):
        below = jnp.where((row < packed) & low, tile, 0.0)
        return jnp.where((row >= packed) & (row < cases) & ~low, pltpu.roll(tile, packed, 0), below)

    def send_force(step, force):
        force_send[step] = jnp.where(low, force, up(force))
        spread_line(lambda px, pk: force_send.at[step, 0:packed], force_recv.at[step], packed, 1 + 2 * step)

    await_near(load_recv.at[0, 0:cases], 0)
    load0 = own_load0 - load_recv[0]
    force = times(load0, (wide_high, wide_low), CONTRACT_LAST)
    send_force(0, force)
    relay("y", ny, 0, 1)
    relay("z", nz, 0, 1)

    get_schur.wait()
    store_split(schur[...], schur_high, schur_low)
    disp0 = times(load0, (schur_high[...], schur_low[...]), CONTRACT)
    disp_send[0] = disp0
    send_near(disp_send.at[0, 0:cases], disp_recv.at[0, 0:cases], 3, left)
    relay("y", ny, 1, ny)
    relay("z", nz, 1, 2)
    await_near(coupling_right, 2)
    next_pair = -times(coupling_right[...], (next_map[...],), CONTRACT)
    for at in range(corners, LANES, half):
        pair_wide[at : at + corners, :] = next_pair
    store_split(pair_wide[...], pair_high, pair_low)

    await_line(index_line, 1, 0)
    index_line[slab] = index_mine[...]
    block_rows = lax.broadcasted_iota(jnp.int32, (block, LANES), 0) + slab * block
    for px in range(nx):
        found = jnp.where(low, index_line[px * nk], index_line[px * nk + 1])[0:1]
        index_rows[px : px + 1, :] = found
        corner_map[:, px * LANES : (px + 1) * LANES] = jnp.where(block_rows == found, 1.0, 0.0).astype(BF16)
    to_smem = pltpu.make_async_copy(index_rows, index_smem, local_sem.at[2])
    to_smem.start()

    def line_force(step):
        await_line(force_recv.at[step], packed, 1 + 2 * step)
        force_recv[step, slab] = force_send[step]
        tiles = []
        for px in range(nx):
            even, odd = force_recv[step, px * nk], force_recv[step, px * nk + 1]
            upper = jnp.where(low, even, pltpu.roll(odd, half, 1))
            lower = pltpu.roll(jnp.where(low, pltpu.roll(even, half, 1), odd), packed, 0)
            tiles.append(jnp.where(row < packed, upper, jnp.where(row < cases, lower, 0.0)))
        return jnp.concatenate(tiles, axis=1)

    def send_picks(step, picks):
        for px in range(nx):
            tile = picks[:, px * LANES : (px + 1) * LANES]
            above = up(tile)
            pick_send[step, px, 0] = jnp.where(low, tile, pltpu.roll(above, half, 1))
            pick_send[step, px, 1] = jnp.where(low, pltpu.roll(tile, half, 1), above)
        spread_line(lambda px, pk: pick_send.at[step, px, pk, 0:packed], pick_recv.at[step], packed, 2 + 2 * step)
        pick_recv[step, slab] = pick_send[step, x, k]

    def get_picks(step):
        await_line(pick_recv.at[step], packed, 2 + 2 * step)
        return unpacked(added(pick_recv.at[step], slabs))

    sum_y0[y] = times(line_force(0), (corner_map[...],), CONTRACT_LAST)
    spread_axis(sum_y0, "y", 0)

    get_inverse.wait()
    to_smem.wait()

    def take(j, carry):
        for px in range(nx):
            for pk in range(nk):
                at = index_smem[px, pk * half + j]
                rows_of[pl.ds(px * LANES + pk * half + j, 1), :] = inverse[pl.ds(at, 1), :]
        return carry

    lax.fori_loop(0, corners, take, 0)
    relay("z", nz, 2, nz)
    await_axis(sum_y0, "y", 0)
    sum_z0[z] = added(sum_y0, ny)
    spread_axis(sum_z0, "z", 1)
    await_near(disp_recv.at[0, 0:cases], 3)
    lax.fori_loop(corners, 2 * corners, take, 0)
    store_split(rows_of[...], rows_high, rows_low)
    local0 = times(disp0, (own_map[...],), CONTRACT) - times(disp_recv[0], (next_map[...],), CONTRACT)
    await_axis(sum_z0, "z", 1)
    total0 = added(sum_z0, nz)
    send_picks(0, times(total0, (rows_high[...], rows_low[...]), CONTRACT_LAST))
    solved0 = get_picks(0)
    image0 = local0 + times(solved0, (pair_high[...], pair_low[...]), CONTRACT)

    scaled = image0 * scale
    send_force(1, times(scaled, (pair_high[...], pair_low[...]), CONTRACT_LAST))
    load_send[1] = times(scaled, (next_map[...],), CONTRACT_LAST)
    send_near(load_send.at[1, 0:cases], load_recv.at[1, 0:cases], 4, right)
    own_load1 = times(scaled, (own_map[...],), CONTRACT_LAST)

    def inner(first_value, second_value):
        return jnp.sum(first_value * second_value, axis=1, keepdims=True)

    start_norm = inner(residual0, direction0)
    curvature = inner(direction0, image0)
    scaled_norm = inner(image0, scaled)
    await_near(load_recv.at[1, 0:cases], 4)
    load1 = own_load1 - load_recv[1]
    disp1 = times(load1, (schur_high[...], schur_low[...]), CONTRACT)
    disp_send[1] = disp1
    send_near(disp_send.at[1, 0:cases], disp_recv.at[1, 0:cases], 5, left)
    energy = inner(load1, disp1)
    sums = jnp.where(
        lane == 0,
        start_norm,
        jnp.where(lane == 1, curvature, jnp.where(lane == 2, scaled_norm, jnp.where(lane == 3, energy, 0.0))),
    )
    forces = line_force(1)
    first_y[y, :, 0:block] = times(forces, (corner_map[...],), CONTRACT_LAST)
    first_y[y, :, block:] = sums
    spread_axis(first_y, "y", 2)
    first_z[z] = times(forces, (rows_high[...], rows_low[...]), CONTRACT)
    spread_axis(first_z, "z", 3)
    await_near(disp_recv.at[1, 0:cases], 5)
    local1 = times(disp1, (own_map[...],), CONTRACT) - times(disp_recv[1], (next_map[...],), CONTRACT)
    await_axis(first_y, "y", 2)
    second_z[z] = added(first_y, ny)
    spread_axis(second_z, "z", 4)
    await_axis(first_z, "z", 3)
    second_y[y] = added(first_z, nz)
    spread_axis(second_y, "y", 5)
    await_axis(second_y, "y", 5)
    solved_block = added(second_y, ny)
    picks = times(solved_block, (corner_map[...],), CONTRACT)
    await_axis(second_z, "z", 4)
    total1 = added(second_z, nz)
    sums = total1[:, block:]
    sums = sums + jnp.where(lane == 3, inner(total1[:, 0:block], solved_block), 0.0)
    spare = half - 16
    sums = pltpu.roll(sums, spare, 1) + pltpu.roll(sums, half + spare, 1)
    send_picks(1, picks + jnp.concatenate([sums] * nx, axis=1))
    solved1 = get_picks(1)
    image1 = local1 + times(solved1, (pair_high[...], pair_low[...]), CONTRACT)

    sums = solved1 + pltpu.roll(solved1, half, 1)
    norm0, curvature, scaled_norm, energy = (sums[:, spare + i : spare + i + 1] for i in range(4))
    alpha0 = norm0 / curvature
    norm1 = alpha0 * alpha0 * scaled_norm - norm0
    ratio = norm1 / norm0
    bent = alpha0 * alpha0 * energy - (norm0 + norm1) * (1.0 + ratio) / alpha0
    alpha1 = norm1 / bent
    residual1 = residual0 - alpha0 * image0
    direction1 = residual1 * scale + ratio * direction0
    along1 = image0 - alpha0 * image1 + ratio * image0
    mult = alpha0 * direction0 + alpha1 * direction1
    res = residual1 - alpha1 * along1
    for i in range(cases):
        out_ref[0, i] = mult[i : i + 1]
        out_ref[1, i] = res[i : i + 1]
    put = fetch(out_ref, out_hbm, 9)
    put.wait()

    for copy in unsent:
        copy.wait_send()


def per_device(ny, nz, nx, nk, jump_data, lumped_scale, schur_inverse, coarse_coupling, corner_inverse, own_dof, nbr_dof, live_count, corner_index):
    cases, records = jump_data.shape[2:]
    corners, iface = coarse_coupling.shape[2:]
    total, block = corner_inverse.shape
    slabs = nx * nk
    wide = nx * LANES
    vmem = lambda *shape: pltpu.VMEM(shape, F32)
    half = lambda *shape: pltpu.VMEM(shape, BF16)
    whole = lambda *shape: pltpu.VMEM(shape, jnp.int32)
    sem = lambda *shape: pltpu.SemaphoreType.DMA(shape)
    in_hbm = pl.BlockSpec(memory_space=pltpu.HBM)
    scratch = [
        vmem(cases, 1, records),
        vmem(1, records),
        vmem(corners, iface),
        whole(1, records),
        whole(1, records),
        whole(1, corners),
        vmem(2, cases, 1, records),
        vmem(iface, iface),
        vmem(total, block),
        half(iface, iface),
        half(iface, iface),
        half(iface, records),
        half(iface, records),
        half(block, wide),
        vmem(wide, block),
        half(wide, block),
        half(wide, block),
        vmem(LANES, iface),
        vmem(LANES, records),
        half(LANES, records),
        half(LANES, records),
        whole(ROWS, LANES),
        whole(ROWS, LANES),
        whole(ROWS, LANES),
        whole(slabs, ROWS, LANES),
        whole(nx, LANES),
        pltpu.SMEM((nx, LANES), jnp.int32),
        vmem(corners, iface),
        vmem(2, ROWS, iface),
        vmem(2, ROWS, iface),
        vmem(2, ROWS, iface),
        vmem(2, ROWS, iface),
        vmem(2, ROWS, LANES),
        vmem(2, slabs, ROWS, LANES),
        vmem(2, nx, nk, ROWS, LANES),
        vmem(2, slabs, ROWS, LANES),
        vmem(ny, ROWS, block),
        vmem(nz, ROWS, block),
        vmem(ny, ROWS, block + LANES),
        vmem(nz, ROWS, block),
        vmem(nz, ROWS, block + LANES),
        vmem(ny, ROWS, block),
        sem(11),
        sem(6),
        sem(6),
        sem(5),
        sem(5),
        sem(6),
        sem(6),
        pltpu.SemaphoreType.REGULAR((3, 4)),
    ]
    outs = pl.pallas_call(
        functools.partial(kernel, ny, nz, nx, nk),
        out_shape=jax.ShapeDtypeStruct((2, cases, 1, records), F32),
        in_specs=[in_hbm] * 6 + [pl.BlockSpec(memory_space=pltpu.SMEM)] + [in_hbm] * 2,
        out_specs=in_hbm,
        scratch_shapes=scratch,
        compiler_params=pltpu.CompilerParams(collective_id=0, has_side_effects=True, vmem_limit_bytes=67043328),
        name="solve",
    )(
        jnp.transpose(jump_data[0], (1, 0, 2)),
        lumped_scale[0],
        coarse_coupling[0, 0],
        own_dof[0],
        nbr_dof[0],
        corner_index[0],
        live_count,
        schur_inverse[0, 0],
        corner_inverse,
    )
    return tuple(jnp.transpose(outs[i], (1, 0, 2))[None] for i in range(2))


def solution(mesh):
    devices = mesh.devices
    sub, crs = devices.shape
    side = 8 if sub == 64 else 2
    ny, nz, nx, nk = side, sub // side, crs // 2, 2
    finer = Mesh(devices.reshape(ny, nz, nx, nk), ("y", "z", "x", "k"))
    SUB, CRS = ("y", "z"), ("x", "k")
    placed = (
        P(SUB, CRS, None, None),
        P(SUB, CRS, None),
        P(SUB, CRS, None, None),
        P(SUB, CRS, None, None),
        P(None, CRS),
        P(SUB, CRS, None),
        P(SUB, CRS, None),
        P(SUB, CRS),
        P(SUB, CRS, None),
    )
    return jax.shard_map(
        functools.partial(per_device, ny, nz, nx, nk),
        mesh=finer,
        in_specs=placed,
        out_specs=(P(SUB, CRS, None, None), P(SUB, CRS, None, None)),
        check_vma=False,
    )
```

```python
import functools

import jax
import jax.numpy as jnp
from jax import lax
from jax.experimental import pallas as pl
from jax.experimental.pallas import tpu as pltpu
from jax.sharding import Mesh
from jax.sharding import PartitionSpec as P

MESH = pl.DeviceIdType.MESH
LANES = 128
ROWS = 8
F32 = jnp.float32
BF16 = jnp.bfloat16
CONTRACT_LAST = (((1,), (1,)), ((), ()))
CONTRACT = (((1,), (0,)), ((), ()))


def parts(value):
    high = value.astype(BF16).astype(F32)
    rest = value - high
    middle = rest.astype(BF16).astype(F32)
    low = rest - middle
    return jnp.concatenate([high, middle, low], axis=0).astype(BF16)


def times(value, matrices, dims):
    rows = value.shape[0]
    stacked = parts(value)
    total = None
    for matrix in matrices:
        found = lax.dot_general(stacked, matrix, dims, preferred_element_type=F32)
        total = found if total is None else total + found
    return total[:rows] + total[rows : 2 * rows] + total[2 * rows :]


def store_split(value, high_ref, low_ref):
    high = value.astype(BF16)
    high_ref[...] = high
    low_ref[...] = (value - high.astype(F32)).astype(BF16)


def kernel(
    ny,
    nz,
    nx,
    nk,
    given_hbm,
    scale_hbm,
    coupling_hbm,
    own_hbm,
    nbr_hbm,
    index_hbm,
    live_ref,
    schur_hbm,
    inverse_hbm,
    out_hbm,
    given_ref,
    scale_ref,
    coupling_ref,
    own_ref,
    nbr_ref,
    index_ref,
    out_ref,
    schur,
    inverse,
    schur_high,
    schur_low,
    own_map,
    next_map,
    corner_map,
    rows_of,
    rows_high,
    rows_low,
    own_wide,
    pair_wide,
    pair_high,
    pair_low,
    index_pad,
    index_right,
    index_mine,
    index_line,
    index_rows,
    index_smem,
    coupling_right,
    load_send,
    load_recv,
    disp_send,
    disp_recv,
    force_send,
    force_recv,
    pick_send,
    pick_recv,
    sum_y0,
    sum_z0,
    first_y,
    first_z,
    second_z,
    second_y,
    local_sem,
    near_send,
    near_recv,
    line_send,
    line_recv,
    axis_send,
    axis_recv,
    relay_sem,
):
    y, z, x, k = (lax.axis_index(a) for a in ("y", "z", "x", "k"))
    slab = x * nk + k
    slabs = nx * nk
    iface = coupling_ref.shape[1]
    corners = coupling_ref.shape[0]
    cases, _, records = given_ref.shape
    block = inverse.shape[1]
    half = LANES // nk

    def plus(value, step, count):
        return lax.rem(value + step + count, count)

    right_z = plus(z, 1, nz)
    right_y = plus(y, jnp.where(z == nz - 1, 1, 0), ny)
    left_z = plus(z, -1, nz)
    left_y = plus(y, jnp.where(z == 0, -1, 0), ny)
    right = {"y": right_y, "z": right_z}
    left = {"y": left_y, "z": left_z}

    def by_distance(count):
        return sorted(range(1, count), key=lambda d: -min(d, count - d))

    line = []
    for dx in sorted(range(nx), key=lambda d: -min(d, nx - d)):
        for dk in range(nk):
            if dx or dk:
                line.append((plus(x, dx, nx), plus(k, dk, nk)))
    ys = [plus(y, d, ny) for d in by_distance(ny)]
    zs = [plus(z, d, nz) for d in by_distance(nz)]

    aside = {
        "x": [{"x": plus(x, d, nx), "k": pk} for d in (-1, 1) for pk in range(nk)],
        "y": [{"y": plus(y, d, ny)} for d in (-1, 1)],
        "z": [{"z": plus(z, d, nz)} for d in (-1, 1)],
    }
    partners = [{"k": plus(k, d, nk)} for d in range(1, nk)]
    barrier = pltpu.get_barrier_semaphore()
    greeted = [left, right] + aside["x"] + aside["y"] + aside["z"] + partners
    for peer in greeted:
        pl.semaphore_signal(barrier, inc=1, device_id=peer, device_id_type=MESH)

    def relay_signal(axis, step):
        for peer in aside[axis]:
            pl.semaphore_signal(relay_sem.at["xyz".index(axis), step], inc=1, device_id=peer, device_id_type=MESH)

    def relay_wait(axis, step):
        pl.semaphore_wait(relay_sem.at["xyz".index(axis), step], len(aside[axis]))

    def relay(axis, count, first_step, last_step):
        for step in range(first_step, last_step):
            if step < count // 2 - 1:
                relay_wait(axis, step)
                if step + 1 < count // 2 - 1:
                    relay_signal(axis, step + 1)

    def fetch(source, target, slot):
        copy = pltpu.make_async_copy(source, target, local_sem.at[slot])
        copy.start()
        return copy

    get_nbr = fetch(nbr_hbm, nbr_ref, 3)
    get_given = fetch(given_hbm, given_ref, 4)
    get_scale = fetch(scale_hbm, scale_ref, 5)
    get_index = fetch(index_hbm, index_ref, 6)
    get_own = fetch(own_hbm, own_ref, 7)
    get_coupling = fetch(coupling_hbm, coupling_ref, 8)

    unsent = []

    def send(source, target, send_sem, recv_sem, device):
        pltpu.make_async_remote_copy(
            src_ref=source,
            dst_ref=target,
            send_sem=send_sem,
            recv_sem=recv_sem,
            device_id=device,
            device_id_type=MESH,
        ).start()

    def bytes_of(view, send_sem, recv_sem):
        return pltpu.make_async_remote_copy(
            src_ref=view,
            dst_ref=view,
            send_sem=send_sem,
            recv_sem=recv_sem,
            device_id=right,
            device_id_type=MESH,
        )

    def send_near(source, target, slot, device):
        send(source, target, near_send.at[slot], near_recv.at[slot], device)
        unsent.append(bytes_of(source, near_send.at[slot], near_recv.at[slot]))

    def await_near(target, slot):
        bytes_of(target, near_send.at[slot], near_recv.at[slot]).wait_recv()

    def spread_line(source_of, target, rows, slot):
        for px, pk in line:
            send(
                source_of(px, pk),
                target.at[slab, 0:rows],
                line_send.at[slot],
                line_recv.at[slot],
                {"x": px, "k": pk},
            )
        unsent.append(bytes_of(target.at[0 : slabs - 1, 0:rows], line_send.at[slot], line_recv.at[slot]))

    def await_line(target, rows, slot):
        bytes_of(target.at[0 : slabs - 1, 0:rows], line_send.at[slot], line_recv.at[slot]).wait_recv()

    def spread_axis(buffer, axis, slot):
        me, peers = (y, ys) if axis == "y" else (z, zs)
        for peer in peers:
            send(buffer.at[me, 0:cases], buffer.at[me, 0:cases], axis_send.at[slot], axis_recv.at[slot], {axis: peer})
        unsent.append(bytes_of(buffer.at[0 : len(peers), 0:cases], axis_send.at[slot], axis_recv.at[slot]))

    def await_axis(buffer, axis, slot):
        peers = ys if axis == "y" else zs
        bytes_of(buffer.at[0 : len(peers), 0:cases], axis_send.at[slot], axis_recv.at[slot]).wait_recv()

    def added(buffer, count):
        total = buffer[0]
        for slot in range(1, count):
            total = total + buffer[slot]
        return total

    def padded(value):
        return jnp.concatenate([value, jnp.zeros((ROWS - value.shape[0], value.shape[1]), F32)], axis=0)

    rows_iface = lax.broadcasted_iota(jnp.int32, (iface, records), 0)
    live_row = lax.broadcasted_iota(jnp.int32, (1, records), 1) < live_ref[0, 0]
    get_nbr.wait()
    get_given.wait()
    get_scale.wait()
    given = jnp.concatenate([given_ref[i] for i in range(cases)], axis=0)
    residual0 = padded(given) * live_row.astype(F32)
    scale = scale_ref[...]
    direction0 = residual0 * scale
    next_map[...] = jnp.where((rows_iface == nbr_ref[...]) & live_row, 1.0, 0.0).astype(BF16)
    load_send[0] = times(direction0, (next_map[...],), CONTRACT_LAST)
    get_index.wait()
    index_pad[...] = jnp.full((ROWS, LANES), -1, jnp.int32)
    index_pad[0:1, 0:corners] = index_ref[...]

    get_own.wait()
    get_coupling.wait()
    pl.semaphore_wait(barrier, len(greeted))
    for axis, count in (("x", nx), ("y", ny), ("z", nz)):
        if count // 2 > 1:
            relay_signal(axis, 0)

    send_near(load_send.at[0, 0:cases], load_recv.at[0, 0:cases], 0, right)
    send_near(index_pad.at[0:1], index_right.at[0:1], 1, left)
    send_near(coupling_ref, coupling_right, 2, left)
    relay("x", nx, 0, 1)

    own_map[...] = jnp.where((rows_iface == own_ref[...]) & live_row, 1.0, 0.0).astype(BF16)
    own_load0 = times(direction0, (own_map[...],), CONTRACT_LAST)
    own_wide[...] = jnp.zeros_like(own_wide)
    pair_wide[...] = jnp.zeros_like(pair_wide)
    rows_of[...] = jnp.zeros_like(rows_of)
    coupling = coupling_ref[...]
    own_pair = times(coupling, (own_map[...],), CONTRACT)
    for at in range(0, LANES, half):
        own_wide[at : at + corners, :] = coupling
        pair_wide[at : at + corners, :] = own_pair
    wide_high = own_wide[...].astype(BF16)
    wide_low = (own_wide[...] - wide_high.astype(F32)).astype(BF16)
    relay("x", nx, 1, nx)

    await_near(index_right.at[0:1], 1)
    lane = lax.broadcasted_iota(jnp.int32, (ROWS, LANES), 1)
    row = lax.broadcasted_iota(jnp.int32, (ROWS, LANES), 0)
    low = lane < half
    both = jnp.where(lane < corners, index_pad[...], pltpu.roll(index_right[...], corners, 1))
    both = jnp.where(lane < 2 * corners, both, -1)
    index_mine[...] = jnp.where(low, both, pltpu.roll(both, half, 1))
    spread_line(lambda px, pk: index_mine.at[0:1], index_line, 1, 0)

    packed = cases // 2

    def up(tile):
        return pltpu.roll(tile, ROWS - packed, 0)

    def unpacked(tile):
        below = jnp.where((row < packed) & low, tile, 0.0)
        return jnp.where((row >= packed) & (row < cases) & ~low, pltpu.roll(tile, packed, 0), below)

    def send_force(step, force):
        force_send[step] = jnp.where(low, force, up(force))
        spread_line(lambda px, pk: force_send.at[step, 0:packed], force_recv.at[step], packed, 1 + 2 * step)

    await_near(load_recv.at[0, 0:cases], 0)
    load0 = own_load0 - load_recv[0]
    force = times(load0, (wide_high, wide_low), CONTRACT_LAST)
    send_force(0, force)
    get_schur = fetch(schur_hbm, schur, 0)
    get_inverse = fetch(inverse_hbm, inverse, 1)
    relay("y", ny, 0, 1)
    relay("z", nz, 0, 1)

    get_schur.wait()
    store_split(schur[...], schur_high, schur_low)
    disp0 = times(load0, (schur_high[...], schur_low[...]), CONTRACT)
    disp_send[0] = disp0
    send_near(disp_send.at[0, 0:cases], disp_recv.at[0, 0:cases], 3, left)
    relay("y", ny, 1, ny)
    relay("z", nz, 1, 2)
    await_near(coupling_right, 2)
    next_pair = -times(coupling_right[...], (next_map[...],), CONTRACT)
    for at in range(corners, LANES, half):
        pair_wide[at : at + corners, :] = next_pair
    store_split(pair_wide[...], pair_high, pair_low)

    await_line(index_line, 1, 0)
    index_line[slab] = index_mine[...]
    block_rows = lax.broadcasted_iota(jnp.int32, (block, LANES), 0) + slab * block
    for px in range(nx):
        found = jnp.where(low, index_line[px * nk], index_line[px * nk + 1])[0:1]
        index_rows[px : px + 1, :] = found
        corner_map[:, px * LANES : (px + 1) * LANES] = jnp.where(block_rows == found, 1.0, 0.0).astype(BF16)
    to_smem = pltpu.make_async_copy(index_rows, index_smem, local_sem.at[2])
    to_smem.start()

    def line_force(step):
        await_line(force_recv.at[step], packed, 1 + 2 * step)
        force_recv[step, slab] = force_send[step]
        tiles = []
        for px in range(nx):
            even, odd = force_recv[step, px * nk], force_recv[step, px * nk + 1]
            upper = jnp.where(low, even, pltpu.roll(odd, half, 1))
            lower = pltpu.roll(jnp.where(low, pltpu.roll(even, half, 1), odd), packed, 0)
            tiles.append(jnp.where(row < packed, upper, jnp.where(row < cases, lower, 0.0)))
        return jnp.concatenate(tiles, axis=1)

    def send_picks(step, picks):
        for px in range(nx):
            tile = picks[:, px * LANES : (px + 1) * LANES]
            above = up(tile)
            pick_send[step, px, 0] = jnp.where(low, tile, pltpu.roll(above, half, 1))
            pick_send[step, px, 1] = jnp.where(low, pltpu.roll(tile, half, 1), above)
        spread_line(lambda px, pk: pick_send.at[step, px, pk, 0:packed], pick_recv.at[step], packed, 2 + 2 * step)
        pick_recv[step, slab] = pick_send[step, x, k]

    def get_picks(step):
        await_line(pick_recv.at[step], packed, 2 + 2 * step)
        return unpacked(added(pick_recv.at[step], slabs))

    sum_y0[y] = times(line_force(0), (corner_map[...],), CONTRACT_LAST)
    spread_axis(sum_y0, "y", 0)

    get_inverse.wait()
    to_smem.wait()

    def take(j, carry):
        for px in range(nx):
            for pk in range(nk):
                at = index_smem[px, pk * half + j]
                rows_of[pl.ds(px * LANES + pk * half + j, 1), :] = inverse[pl.ds(at, 1), :]
        return carry

    lax.fori_loop(0, corners, take, 0)
    relay("z", nz, 2, nz)
    await_axis(sum_y0, "y", 0)
    sum_z0[z] = added(sum_y0, ny)
    spread_axis(sum_z0, "z", 1)
    await_near(disp_recv.at[0, 0:cases], 3)
    lax.fori_loop(corners, 2 * corners, take, 0)
    store_split(rows_of[...], rows_high, rows_low)
    local0 = times(disp0, (own_map[...],), CONTRACT) - times(disp_recv[0], (next_map[...],), CONTRACT)
    await_axis(sum_z0, "z", 1)
    total0 = added(sum_z0, nz)
    send_picks(0, times(total0, (rows_high[...], rows_low[...]), CONTRACT_LAST))
    solved0 = get_picks(0)
    image0 = local0 + times(solved0, (pair_high[...], pair_low[...]), CONTRACT)

    scaled = image0 * scale
    send_force(1, times(scaled, (pair_high[...], pair_low[...]), CONTRACT_LAST))
    load_send[1] = times(scaled, (next_map[...],), CONTRACT_LAST)
    send_near(load_send.at[1, 0:cases], load_recv.at[1, 0:cases], 4, right)
    own_load1 = times(scaled, (own_map[...],), CONTRACT_LAST)

    def inner(first_value, second_value):
        return jnp.sum(first_value * second_value, axis=1, keepdims=True)

    start_norm = inner(residual0, direction0)
    curvature = inner(direction0, image0)
    scaled_norm = inner(image0, scaled)
    await_near(load_recv.at[1, 0:cases], 4)
    load1 = own_load1 - load_recv[1]
    disp1 = times(load1, (schur_high[...], schur_low[...]), CONTRACT)
    disp_send[1] = disp1
    send_near(disp_send.at[1, 0:cases], disp_recv.at[1, 0:cases], 5, left)
    energy = inner(load1, disp1)
    sums = jnp.where(
        lane == 0,
        start_norm,
        jnp.where(lane == 1, curvature, jnp.where(lane == 2, scaled_norm, jnp.where(lane == 3, energy, 0.0))),
    )
    forces = line_force(1)
    first_y[y, :, 0:block] = times(forces, (corner_map[...],), CONTRACT_LAST)
    first_y[y, :, block:] = sums
    spread_axis(first_y, "y", 2)
    first_z[z] = times(forces, (rows_high[...], rows_low[...]), CONTRACT)
    spread_axis(first_z, "z", 3)
    await_near(disp_recv.at[1, 0:cases], 5)
    local1 = times(disp1, (own_map[...],), CONTRACT) - times(disp_recv[1], (next_map[...],), CONTRACT)
    await_axis(first_y, "y", 2)
    second_z[z] = added(first_y, ny)
    spread_axis(second_z, "z", 4)
    await_axis(first_z, "z", 3)
    second_y[y] = added(first_z, nz)
    spread_axis(second_y, "y", 5)
    await_axis(second_y, "y", 5)
    solved_block = added(second_y, ny)
    picks = times(solved_block, (corner_map[...],), CONTRACT)
    await_axis(second_z, "z", 4)
    total1 = added(second_z, nz)
    sums = total1[:, block:]
    sums = sums + jnp.where(lane == 3, inner(total1[:, 0:block], solved_block), 0.0)
    spare = half - 16
    sums = pltpu.roll(sums, spare, 1) + pltpu.roll(sums, half + spare, 1)
    send_picks(1, picks + jnp.concatenate([sums] * nx, axis=1))
    solved1 = get_picks(1)
    image1 = local1 + times(solved1, (pair_high[...], pair_low[...]), CONTRACT)

    sums = solved1 + pltpu.roll(solved1, half, 1)
    norm0, curvature, scaled_norm, energy = (sums[:, spare + i : spare + i + 1] for i in range(4))
    alpha0 = norm0 / curvature
    norm1 = alpha0 * alpha0 * scaled_norm - norm0
    ratio = norm1 / norm0
    bent = alpha0 * alpha0 * energy - (norm0 + norm1) * (1.0 + ratio) / alpha0
    alpha1 = norm1 / bent
    residual1 = residual0 - alpha0 * image0
    direction1 = residual1 * scale + ratio * direction0
    along1 = image0 - alpha0 * image1 + ratio * image0
    mult = alpha0 * direction0 + alpha1 * direction1
    res = residual1 - alpha1 * along1
    for i in range(cases):
        out_ref[0, i] = mult[i : i + 1]
        out_ref[1, i] = res[i : i + 1]
    put = fetch(out_ref, out_hbm, 9)
    put.wait()

    for copy in unsent:
        copy.wait_send()


def per_device(ny, nz, nx, nk, jump_data, lumped_scale, schur_inverse, coarse_coupling, corner_inverse, own_dof, nbr_dof, live_count, corner_index):
    cases, records = jump_data.shape[2:]
    corners, iface = coarse_coupling.shape[2:]
    total, block = corner_inverse.shape
    slabs = nx * nk
    wide = nx * LANES
    vmem = lambda *shape: pltpu.VMEM(shape, F32)
    half = lambda *shape: pltpu.VMEM(shape, BF16)
    whole = lambda *shape: pltpu.VMEM(shape, jnp.int32)
    sem = lambda *shape: pltpu.SemaphoreType.DMA(shape)
    in_hbm = pl.BlockSpec(memory_space=pltpu.HBM)
    scratch = [
        vmem(cases, 1, records),
        vmem(1, records),
        vmem(corners, iface),
        whole(1, records),
        whole(1, records),
        whole(1, corners),
        vmem(2, cases, 1, records),
        vmem(iface, iface),
        vmem(total, block),
        half(iface, iface),
        half(iface, iface),
        half(iface, records),
        half(iface, records),
        half(block, wide),
        vmem(wide, block),
        half(wide, block),
        half(wide, block),
        vmem(LANES, iface),
        vmem(LANES, records),
        half(LANES, records),
        half(LANES, records),
        whole(ROWS, LANES),
        whole(ROWS, LANES),
        whole(ROWS, LANES),
        whole(slabs, ROWS, LANES),
        whole(nx, LANES),
        pltpu.SMEM((nx, LANES), jnp.int32),
        vmem(corners, iface),
        vmem(2, ROWS, iface),
        vmem(2, ROWS, iface),
        vmem(2, ROWS, iface),
        vmem(2, ROWS, iface),
        vmem(2, ROWS, LANES),
        vmem(2, slabs, ROWS, LANES),
        vmem(2, nx, nk, ROWS, LANES),
        vmem(2, slabs, ROWS, LANES),
        vmem(ny, ROWS, block),
        vmem(nz, ROWS, block),
        vmem(ny, ROWS, block + LANES),
        vmem(nz, ROWS, block),
        vmem(nz, ROWS, block + LANES),
        vmem(ny, ROWS, block),
        sem(11),
        sem(6),
        sem(6),
        sem(5),
        sem(5),
        sem(6),
        sem(6),
        pltpu.SemaphoreType.REGULAR((3, 4)),
    ]
    outs = pl.pallas_call(
        functools.partial(kernel, ny, nz, nx, nk),
        out_shape=jax.ShapeDtypeStruct((2, cases, 1, records), F32),
        in_specs=[in_hbm] * 6 + [pl.BlockSpec(memory_space=pltpu.SMEM)] + [in_hbm] * 2,
        out_specs=in_hbm,
        scratch_shapes=scratch,
        compiler_params=pltpu.CompilerParams(collective_id=0, has_side_effects=True, vmem_limit_bytes=67043328),
        name="solve",
    )(
        jnp.transpose(jump_data[0], (1, 0, 2)),
        lumped_scale[0],
        coarse_coupling[0, 0],
        own_dof[0],
        nbr_dof[0],
        corner_index[0],
        live_count,
        schur_inverse[0, 0],
        corner_inverse,
    )
    return tuple(jnp.transpose(outs[i], (1, 0, 2))[None] for i in range(2))


def solution(mesh):
    devices = mesh.devices
    sub, crs = devices.shape
    side = 8 if sub == 64 else 2
    ny, nz, nx, nk = side, sub // side, crs // 2, 2
    finer = Mesh(devices.reshape(ny, nz, nx, nk), ("y", "z", "x", "k"))
    SUB, CRS = ("y", "z"), ("x", "k")
    placed = (
        P(SUB, CRS, None, None),
        P(SUB, CRS, None),
        P(SUB, CRS, None, None),
        P(SUB, CRS, None, None),
        P(None, CRS),
        P(SUB, CRS, None),
        P(SUB, CRS, None),
        P(SUB, CRS),
        P(SUB, CRS, None),
    )
    return jax.shard_map(
        functools.partial(per_device, ny, nz, nx, nk),
        mesh=finer,
        in_specs=placed,
        out_specs=(P(SUB, CRS, None, None), P(SUB, CRS, None, None)),
        check_vma=False,
    )
```
